32 devices in a mesh: dir: 2 (over x), gz: 8 (over z, y), gy: 2 (over core).
Axes of the slice: x: 2, y: 2, z: 4, core: 2. Of those that a mesh axis runs over, the one named last changes fastest.
Arguments:
- estimate: bfloat16 [96, 64, 128, 128], P('dir', 'gz', 'gy'), may hold values from -6 to 6
- observed: bfloat16 [96, 64, 128, 128], P('dir', 'gz', 'gy'), may hold values from -6 to 6
- profile_weight: float32 [17], replicated, may hold values from 0.02 to 0.12
- band_offset: int32 [17], replicated, may hold values from -8 to 8, as said below
- slab_shot: int32 [8], replicated, may hold values from 0 to 3
- shot_gain: float32 [4, 96], P(None, 'dir'), may hold values from 0.1 to 1.9
- fit_matrix: bfloat16 [96, 45], replicated, may hold values from -0.625 to 0.625
- basis: bfloat16 [45, 96], replicated, may hold values from -0.875 to 0.875
Outputs:
- correction: bfloat16 [96, 64, 128, 128], P('dir', 'gz', 'gy')
- updated: bfloat16 [96, 64, 128, 128], P('dir', 'gz', 'gy')
The draws below stay inside these ranges and needn't reach their ends.
Inputs may be any that keep to these rules, and one draw needn't show every extreme that they name: `band_offset`: the first tap's offset is -8 and the last tap's is 8.
All inputs are finite; a program needn't handle non-finite values.
Results may differ from the reference program's by a relative error of at most 0.0055.
Values may be sent and summed in bfloat16 or wider, within the bound.
A program may use at most 128 MiB of HBM per device.

```python
import jax
import jax.numpy as jnp
from jax import lax

NDIR = 96
NCOEF = 45
TAPS = 17
HALO = 8
SLAB = 8
SHOTS = 4
NX = 128
NZ = 64
NY = 128
SLABS = 8


def draw_band_offset(key, part):
    middle = jax.random.randint(key, (TAPS - 2,), -HALO, HALO + 1).astype(jnp.int32)
    first = jnp.full((1,), -HALO, jnp.int32)
    last = jnp.full((1,), HALO, jnp.int32)
    return jnp.concatenate([first, middle, last])


def plant(drawn, rng, smallest, high):
    extent = drawn.shape
    index_at = [jax.random.randint(jax.random.fold_in(rng, axis), (), 0, extent[axis]) for axis in range(len(extent))]
    drawn = drawn.at[tuple(index_at)].set(smallest)
    longest = extent.index(max(extent))
    index_at[longest] = (index_at[longest] + 1) % extent[longest]
    return drawn.at[tuple(index_at)].set(high)


def block_scale(key, dims, pieces, smallest, high):
    level, own = 1.0, jax.random.fold_in(key, 6)
    for dim, shards_of in pieces:
        heights = jnp.exp(jax.random.uniform(jax.random.fold_in(own, dim), (shards_of,), jnp.float32, smallest / len(pieces), high / len(pieces)))
        level = level * jnp.repeat(heights, dims[dim] // shards_of).reshape([-1 if axis == dim else 1 for axis in range(len(dims))])
    return level


def bell_draw(own_key, shape, width, bound, pieces=(), kind=jnp.bfloat16):
    values = jax.random.normal(own_key, shape, jnp.float32) * width
    if len(pieces) > 0:
        values = block_scale(own_key, shape, pieces, -0.22, 0.18) * values
    return jnp.clip(values, min=-bound, max=bound).astype(kind)


def setup_inputs(seed: int = 0) -> dict:
    keys = jax.random.split(jax.random.key(seed), 9)
    return {
        "estimate": bell_draw(keys[0], (NDIR, NZ, NY, NX), 1.0, 6.0, ((0, 2), (1, 8), (2, 2))),
        "observed": bell_draw(keys[1], (NDIR, NZ, NY, NX), 1.0, 6.0, ((0, 2), (1, 8), (2, 2))),
        "profile_weight": jnp.clip(jax.random.uniform(keys[2], (TAPS,), jnp.float32, 0.02, 0.12), 0.02, 0.12),
        "band_offset": draw_band_offset(jax.random.fold_in(keys[8], 71), 0),
        "slab_shot": plant(jax.random.randint(keys[4], (SLABS,), 0, SHOTS), jax.random.fold_in(keys[4], 1), 0, SHOTS - 1).astype(jnp.int32),
        "shot_gain": jnp.clip(1.0 + 0.18 * jax.random.normal(keys[5], (SHOTS, NDIR), jnp.float32), 0.1, 1.9),
        "fit_matrix": bell_draw(keys[6], (NDIR, NCOEF), NDIR ** -0.5, 0.625),
        "basis": bell_draw(keys[7], (NCOEF, NDIR), NCOEF ** -0.5, 0.875),
    }


STEP_SIZE = 0.5


def band_sum(padded, weights, offsets, sign, count, axis):
    total = jnp.zeros(padded.shape[:axis] + (count,) + padded.shape[axis + 1:], jnp.float32)
    for tap in range(TAPS):
        start = (HALO + sign * offsets[tap]).astype(jnp.int32)
        piece = lax.dynamic_slice_in_dim(padded, start, count, axis)
        total = total + weights[tap] * piece.astype(jnp.float32)
    return total


def reference(estimate, observed, profile_weight, band_offset, slab_shot, shot_gain, fit_matrix, basis):
    depth = jnp.arange(NZ, dtype=jnp.int32) // SLAB
    slab_hit = (depth[:, None] == jnp.arange(SLABS, dtype=jnp.int32)[None, :]).astype(jnp.int32)
    shot_of_z = jnp.sum(slab_hit * slab_shot[None, :], axis=1)
    shot_hit = (shot_of_z[:, None] == jnp.arange(SHOTS, dtype=jnp.int32)[None, :]).astype(jnp.float32)
    gain = jnp.sum(shot_hit[:, :, None] * shot_gain[None, :, :], axis=1)

    def one_direction(item):
        volume, seen, scale = item
        padded = jnp.pad(volume.astype(jnp.float32), ((HALO, HALO), (0, 0), (0, 0)))
        blurred = band_sum(padded, profile_weight, band_offset, 1, NZ, 0)
        scale = scale[:, None, None]
        return (scale * (seen.astype(jnp.float32) - scale * blurred)).astype(jnp.bfloat16)

    residual = lax.map(one_direction, (estimate, observed, gain.T))
    by_depth = jnp.moveaxis(residual, 1, 0)

    def fit_depth(rows):
        flat = rows.reshape(NDIR, NY * NX)
        fitted = jnp.dot(fit_matrix.T, flat, preferred_element_type=jnp.float32)
        return fitted.astype(jnp.bfloat16).reshape(NCOEF, NY, NX)

    coeffs = lax.map(fit_depth, by_depth)
    padded = jnp.pad(coeffs.astype(jnp.float32), ((HALO, HALO), (0, 0), (0, 0), (0, 0)))
    filtered = band_sum(padded, profile_weight, band_offset, -1, NZ, 0)
    basis_wide = basis.T.astype(jnp.float32)

    def synth_depth(rows):
        flat = rows.reshape(NCOEF, NY * NX)
        made = jnp.dot(basis_wide, flat, precision=lax.Precision.HIGHEST)
        return made.astype(jnp.bfloat16).reshape(NDIR, NY, NX)

    correction = jnp.moveaxis(lax.map(synth_depth, filtered), 0, 1)
    updated = (estimate.astype(jnp.float32) + STEP_SIZE * correction.astype(jnp.float32)).astype(jnp.bfloat16)
    return (correction, updated)
```

```python
import functools

import jax
import jax.numpy as jnp
from jax import lax
from jax.experimental import pallas as pl
from jax.experimental.pallas import tpu as pltpu
from jax.sharding import PartitionSpec as P

HALO = 8
SLAB = 8
STEP_SIZE = 0.5
CHUNKS = 2


def divisor(count, most):
    return max(size for size in range(1, most + 1) if count % size == 0)


def band_terms(weights, pieces, depth):
    sums = [None] * (2 * depth)
    for place in range(4 * depth):
        source = pieces[place // depth]
        if source is None:
            continue
        plane = source(place % depth).astype(jnp.float32)
        for out in range(2 * depth):
            tap = place - depth - out + HALO
            if 0 <= tap <= 2 * HALO:
                term = weights[tap] * plane
                sums[out] = term if sums[out] is None else sums[out] + term
    return sums


def in_order(odd_ref, body):
    @pl.when(odd_ref[0] == 0)
    def _():
        body((0, 1, 2, 3))

    @pl.when(odd_ref[0] == 1)
    def _():
        body((3, 2, 1, 0))


def residual_kernel(odd, taps, gains, far_a, far_b, kept, got, seen_kept, seen_got, out):
    block, depth = kept.shape[:2]
    first = pl.program_id(0) * block
    weights = [taps[i] for i in range(2 * HALO + 1)]
    refs = (far_b, kept, got, far_a)
    seen = (None, seen_kept, seen_got, None)

    def body(order):
        def one(d, carry):
            pieces = [lambda z, ref=refs[i]: ref[d, z] for i in order]
            sums = band_terms(weights, pieces, depth)
            for half in range(2):
                which = order[1 + half]
                scale = gains[which - 1, first + d]
                for z in range(depth):
                    value = seen[which][d, z].astype(jnp.float32) - scale * sums[half * depth + z]
                    out[d, which - 1, z] = (scale * value).astype(out.dtype)
            return carry

        lax.fori_loop(0, block, one, 0)

    in_order(odd, body)


def filter_kernel(odd, taps, far_a, far_b, kept, got, out_kept, out_got):
    block, depth = kept.shape[:2]
    weights = [taps[i] for i in range(2 * HALO + 1)]
    refs = (far_b, kept, got, far_a)
    outs = (None, out_kept, out_got, None)

    def body(order):
        def one(c, carry):
            pieces = [lambda z, ref=refs[i]: ref[c, z] for i in order]
            sums = band_terms(weights, pieces, depth)
            for half in range(2):
                for z in range(depth):
                    outs[order[1 + half]][c, z] = sums[half * depth + z].astype(out_kept.dtype)
            return carry

        lax.fori_loop(0, block, one, 0)

    in_order(odd, body)


def plane_call(kernel, scalars, arrays, outs, most):
    count = arrays[0].shape[0]
    block = divisor(count, most)

    def spec(shape):
        return pl.BlockSpec((block,) + shape[1:], lambda i, rest=len(shape) - 1: (i,) + (0,) * rest)

    moved = sum(a.size for a in arrays) * 2 + sum(o.size for o in outs) * 2
    return pl.pallas_call(
        kernel,
        grid=(count // block,),
        in_specs=[pl.BlockSpec(memory_space=pltpu.SMEM)] * len(scalars)
        + [spec(a.shape) for a in arrays],
        out_specs=[spec(o.shape) for o in outs],
        out_shape=outs,
        cost_estimate=pl.CostEstimate(
            flops=34 * sum(o.size for o in outs), bytes_accessed=moved, transcendentals=0
        ),
    )(*scalars, *arrays)


def shards(
    estimate, observed, profile_weight, band_offset, slab_shot, shot_gain, fit_matrix, basis
):
    dirs, depth, rows, width = estimate.shape
    slabs = lax.axis_size("gz")
    parts = lax.axis_size("dir")
    slab = lax.axis_index("gz")
    part = lax.axis_index("dir")
    odd = slab % 2
    flag = odd.astype(jnp.int32).reshape(1)

    spread = jnp.arange(-HALO, HALO + 1, dtype=jnp.int32)
    hit = (band_offset[None, :] == spread[:, None]).astype(jnp.float32)
    taps = jnp.sum(hit * profile_weight[None, :], axis=1)

    def gain_of(which):
        index = slab_shot[(which * depth) // SLAB]
        shot_hit = (jnp.arange(shot_gain.shape[0], dtype=jnp.int32) == index).astype(jnp.float32)
        return jnp.sum(shot_hit[:, None] * shot_gain, axis=0)

    gains = jnp.stack([gain_of(slab), gain_of(slab + 1 - 2 * odd)])

    pair = [(i, i ^ 1) for i in range(slabs)]
    away = [(i, i - 2 if i % 2 == 0 else i + 2) for i in range(slabs)]
    away = [(i, j) for i, j in away if 0 <= j < slabs]
    across = [(i, i + 2 if i % 2 == 0 else i - 2) for i in range(slabs)]
    across = [(i, j) for i, j in across if 0 <= j < slabs]

    half = rows // 2
    tile = half // CHUNKS
    strip = tile // parts
    first = lax.rem(part + jnp.arange(parts, dtype=jnp.int32) * (parts - 1), parts)

    def swap_rows(cells, chunk):
        keep = lax.dynamic_slice_in_dim(cells, odd * half + chunk * tile, tile, 2)
        send = lax.dynamic_slice_in_dim(cells, (1 - odd) * half + chunk * tile, tile, 2)
        return keep, lax.ppermute(send, "gz", pair)

    stage = []
    for chunk in range(CHUNKS):
        kept, got = swap_rows(estimate, chunk)
        far_a = lax.ppermute(kept, "gz", away)
        seen_kept, seen_got = swap_rows(observed, chunk)
        far_b = lax.ppermute(got, "gz", across)
        stage.append((far_a, far_b, kept, got, seen_kept, seen_got))

    fit_rows = fit_matrix.reshape(parts, dirs, -1)[first].reshape(parts * dirs, -1)
    strips = []
    for chunk in range(CHUNKS):
        (residual,) = plane_call(
            residual_kernel,
            (flag, taps, gains),
            stage[chunk],
            [jax.ShapeDtypeStruct((dirs, 2, depth, tile, width), jnp.bfloat16)],
            8,
        )
        found = []
        for hop in range(parts):
            target = lax.rem(part + hop, parts)
            piece = lax.dynamic_slice_in_dim(residual, target * strip, strip, 3)
            if hop:
                piece = lax.ppermute(
                    piece, "dir", [(i, (i + hop) % parts) for i in range(parts)]
                )
            found.append(piece)
        voxels = jnp.concatenate(found, axis=0)
        coeffs = jnp.einsum(
            "dszyx,dc->sczyx", voxels, fit_rows, preferred_element_type=jnp.float32
        ).astype(jnp.bfloat16)
        kept, got = coeffs[0], coeffs[1]
        far_a = lax.ppermute(kept, "gz", away)
        far_b = lax.ppermute(got, "gz", across)
        shape = jax.ShapeDtypeStruct(kept.shape, jnp.bfloat16)
        mine, other = plane_call(
            filter_kernel, (flag, taps[::-1]), (far_a, far_b, kept, got), [shape, shape], 9
        )
        other = lax.ppermute(other, "gz", pair)
        both = []
        for piece in (mine, other):
            ring = [piece] + [
                lax.ppermute(piece, "dir", [(i, (i + hop) % parts) for i in range(parts)])
                for hop in range(1, parts)
            ]
            if parts == 2:
                low = jnp.where(part == 0, ring[0], ring[1])
                high = jnp.where(part == 0, ring[1], ring[0])
                both.append(jnp.concatenate([low, high], axis=2))
            else:
                stacked = jnp.stack(ring)
                order = lax.rem(part - jnp.arange(parts, dtype=jnp.int32) + parts, parts)
                both.append(jnp.concatenate(list(stacked[order]), axis=2))
        strips.append(both)

    mine = jnp.concatenate([both[0] for both in strips], axis=2)
    other = jnp.concatenate([both[1] for both in strips], axis=2)
    filtered = jnp.concatenate(
        [jnp.where(odd == 0, mine, other), jnp.where(odd == 0, other, mine)], axis=2
    )
    own_basis = lax.dynamic_slice_in_dim(basis, part * dirs, dirs, 1)
    correction = jnp.einsum(
        "czyx,cd->dzyx", filtered, own_basis, preferred_element_type=jnp.float32
    ).astype(jnp.bfloat16)
    updated = (estimate.astype(jnp.float32) + STEP_SIZE * correction.astype(jnp.float32)).astype(
        jnp.bfloat16
    )
    return (correction, updated)


def solution(mesh):
    return jax.shard_map(
        shards,
        mesh=mesh,
        in_specs=(
            P("dir", "gz", "gy", None),
            P("dir", "gz", "gy", None),
            P(),
            P(),
            P(),
            P(None, "dir"),
            P(),
            P(),
        ),
        out_specs=(P("dir", "gz", "gy", None), P("dir", "gz", "gy", None)),
        check_vma=False,
    )
```

```python
import functools

import jax
import jax.numpy as jnp
from jax import lax
from jax.experimental import pallas as pl
from jax.experimental.pallas import tpu as pltpu
from jax.sharding import PartitionSpec as P

HALO = 8
SLAB = 8
STEP_SIZE = 0.5
CHUNKS = 2
SPLIT = 2


def divisor(count, most):
    return max(size for size in range(1, most + 1) if count % size == 0)


def band_terms(weights, pieces, depth):
    sums = [None] * (2 * depth)
    for place in range(4 * depth):
        plane = pieces[place // depth](place % depth).astype(jnp.float32)
        for out in range(2 * depth):
            tap = place - depth - out + HALO
            if 0 <= tap <= 2 * HALO:
                term = weights[tap] * plane
                sums[out] = term if sums[out] is None else sums[out] + term
    return sums


def in_order(odd, body):
    @pl.when(odd == 0)
    def _():
        body((0, 1, 2, 3))

    @pl.when(odd == 1)
    def _():
        body((3, 2, 1, 0))


def residual_kernel(start, where, taps, gains, far_a, far_b, kept, got, seen_kept, seen_got, out):
    block, depth = kept.shape[:2]
    weights = [taps[i] for i in range(2 * HALO + 1)]
    first = (pl.program_id(0) + start) * block
    refs = (far_b, kept, got, far_a)
    seen = (None, seen_kept, seen_got, None)

    def body(order):
        def one(d, carry):
            pieces = [lambda z, ref=refs[i]: ref[d, z] for i in order]
            sums = band_terms(weights, pieces, depth)
            for half in range(2):
                which = order[1 + half]
                scale = gains[which - 1, first + d]
                for z in range(depth):
                    value = seen[which][d, z].astype(jnp.float32) - scale * sums[half * depth + z]
                    out[d, which - 1, z] = (scale * value).astype(out.dtype)
            return carry

        lax.fori_loop(0, block, one, 0)

    in_order(where[0], body)


def filter_kernel(where, taps, far_a, far_b, kept, got, out_kept, out_got):
    block, depth = kept.shape[:2]
    weights = [taps[i] for i in range(2 * HALO + 1)]
    refs = (far_b, kept, got, far_a)
    outs = (None, out_kept, out_got, None)

    def body(order):
        def one(c, carry):
            pieces = [lambda z, ref=refs[i]: ref[c, z] for i in order]
            sums = band_terms(weights, pieces, depth)
            for half in range(2):
                for z in range(depth):
                    outs[order[1 + half]][c, z] = sums[half * depth + z].astype(out_kept.dtype)
            return carry

        lax.fori_loop(0, block, one, 0)

    in_order(where[0], body)


def finish_kernel(where, made, estimate, *refs):
    correction, updated = refs[-2:]
    value = made[...]
    correction[...] = value
    updated[...] = (
        estimate[...].astype(jnp.float32) + STEP_SIZE * value.astype(jnp.float32)
    ).astype(updated.dtype)


def estimate_cost(arrays, flops):
    return pl.CostEstimate(flops=flops, bytes_accessed=sum(arrays) * 2, transcendentals=0)


def residual_call(where, taps, gains, arrays, seen, strip, start, count):
    depth, width = arrays[0].shape[1], arrays[0].shape[3]
    if strip % 8:
        rows = where[1] * strip
        arrays = [lax.dynamic_slice_in_dim(a, rows, strip, 2) for a in arrays]
        seen = [lax.dynamic_slice_in_dim(a, rows, strip, 2) for a in seen]
        where = where * jnp.array([1, 0], jnp.int32)
    block = divisor(count, 8)
    begin = start // block
    shape = (block, depth, strip, width)
    whole = pl.BlockSpec(shape, lambda i, w: (i + begin, 0, w[1], 0))
    part = pl.BlockSpec(shape, lambda i, w: (i, 0, w[1], 0))
    size = count * depth * strip * width
    return pl.pallas_call(
        functools.partial(residual_kernel, begin),
        grid_spec=pltpu.PrefetchScalarGridSpec(
            num_scalar_prefetch=1,
            grid=(count // block,),
            in_specs=[pl.BlockSpec(memory_space=pltpu.SMEM)] * 2 + [whole] * 4 + [part] * 2,
            out_specs=pl.BlockSpec(
                (block, 2, depth, strip, width), lambda i, w: (i, 0, 0, 0, 0)
            ),
        ),
        out_shape=jax.ShapeDtypeStruct((count, 2, depth, strip, width), jnp.bfloat16),
        cost_estimate=estimate_cost([size * 8], 70 * size),
    )(where, taps, gains, *arrays, *seen)


def filter_call(where, taps, arrays):
    count, depth, strip, width = arrays[0].shape
    block = divisor(count, 9)
    spec = pl.BlockSpec((block, depth, strip, width), lambda i, w: (i, 0, 0, 0))
    shape = jax.ShapeDtypeStruct(arrays[0].shape, jnp.bfloat16)
    return pl.pallas_call(
        filter_kernel,
        grid_spec=pltpu.PrefetchScalarGridSpec(
            num_scalar_prefetch=1,
            grid=(count // block,),
            in_specs=[pl.BlockSpec(memory_space=pltpu.SMEM)] + [spec] * 4,
            out_specs=[spec, spec],
        ),
        out_shape=[shape, shape],
        cost_estimate=estimate_cost([a.size for a in arrays] * 2, 70 * arrays[0].size),
    )(where, taps, *arrays)


def finish_call(number, made, estimate, outs):
    count, depth, strip, width = made.shape
    block = divisor(count, 8)
    spec = pl.BlockSpec((block, depth, strip, width), lambda i, w: (i, 0, 0, 0))
    place = pl.BlockSpec((block, depth, strip, width), lambda i, w: (i, 0, w[0], 0))
    shape = jax.ShapeDtypeStruct(estimate.shape, estimate.dtype)
    return pl.pallas_call(
        finish_kernel,
        grid_spec=pltpu.PrefetchScalarGridSpec(
            num_scalar_prefetch=1,
            grid=(count // block,),
            in_specs=[spec, place] + [pl.BlockSpec(memory_space=pl.ANY)] * len(outs),
            out_specs=[place, place],
        ),
        out_shape=[shape, shape],
        input_output_aliases={3: 0, 4: 1} if outs else {},
        cost_estimate=estimate_cost([made.size * 4], 4 * made.size),
    )(number, made, estimate, *outs)


def shards(
    estimate, observed, profile_weight, band_offset, slab_shot, shot_gain, fit_matrix, basis
):
    dirs, depth, rows, width = estimate.shape
    slabs = lax.axis_size("gz")
    parts = lax.axis_size("dir")
    slab = lax.axis_index("gz").astype(jnp.int32)
    part = lax.axis_index("dir").astype(jnp.int32)
    odd = slab % 2

    pair = [(i, i ^ 1) for i in range(slabs)]

    def inside(moves):
        return [(i, j) for i, j in moves if 0 <= j < slabs]

    away = inside([(i, i - 2 if i % 2 == 0 else i + 2) for i in range(slabs)])
    across = inside([(i, i + 2 if i % 2 == 0 else i - 2) for i in range(slabs)])

    spread = jnp.arange(-HALO, HALO + 1, dtype=jnp.int32)
    hit = (band_offset[None, :] == spread[:, None]).astype(jnp.float32)
    forward = jnp.sum(hit * profile_weight[None, :], axis=1)
    back = forward[::-1]

    def gain_of(which):
        index = slab_shot[(which * depth) // SLAB]
        shot_hit = (jnp.arange(shot_gain.shape[0], dtype=jnp.int32) == index).astype(jnp.float32)
        return jnp.sum(shot_hit[:, None] * shot_gain, axis=0)

    gains = jnp.stack([gain_of(slab), gain_of(slab + 1 - 2 * odd)])

    half = rows // 2
    tile = half // CHUNKS
    strip = tile // parts
    some = dirs // SPLIT
    first = lax.rem(part + jnp.arange(parts, dtype=jnp.int32) * (parts - 1), parts)
    fit_rows = fit_matrix.reshape(parts, SPLIT, some, -1)[first]
    fit_rows = jnp.swapaxes(fit_rows, 0, 1).reshape(parts * dirs, -1)
    own_basis = lax.dynamic_slice_in_dim(basis, part * dirs, dirs, 1)

    def rows_of(cells, side, chunk):
        return lax.dynamic_slice_in_dim(cells, side * half + chunk * tile, tile, 2)

    def scoped(name, *args):
        with jax.named_scope(name):
            return lax.ppermute(*args)

    stage = []
    source, seen_source = estimate, observed
    for chunk in range(CHUNKS):
        send = rows_of(source, 1 - odd, chunk)
        got = scoped(f"est{chunk}", send, "gz", pair)
        kept = rows_of(source, odd, chunk)
        far_a = lax.ppermute(kept, "gz", away)
        seen_source, _ = lax.optimization_barrier((seen_source, send))
        seen_send = rows_of(seen_source, 1 - odd, chunk)
        seen = []
        for piece in range(SPLIT):
            cut = lax.slice_in_dim(seen_send, piece * some, (piece + 1) * some, axis=0)
            arrived = scoped(f"obs{chunk}p{piece}", cut, "gz", pair)
            kept_cut = lax.dynamic_slice(
                seen_source,
                (piece * some, 0, odd * half + chunk * tile, 0),
                (some, depth, tile, width),
            )
            seen.append((kept_cut, arrived))
        source, _ = lax.optimization_barrier((source, seen_send))
        far_b = lax.ppermute(got, "gz", across)
        stage.append(((far_a, far_b, kept, got), seen))

    outs = ()
    if strip % 8:
        outs = (jnp.zeros_like(estimate),)
    for chunk in range(CHUNKS):
        arrays, seen = stage[chunk]
        found = []
        for piece in range(SPLIT):
            sent = []
            for hop in list(range(1, parts)) + [0]:
                where = jnp.stack([odd, lax.rem(part + hop, parts)])
                residual = residual_call(
                    where, forward, gains, arrays, seen[piece], strip, piece * some, some
                )
                if hop:
                    residual = scoped(
                        f"res{chunk}p{piece}",
                        residual,
                        "dir",
                        [(i, (i + hop) % parts) for i in range(parts)],
                    )
                sent.append(residual)
            found += sent[-1:] + sent[:-1]
        voxels = jnp.concatenate(found, axis=0)
        coeffs = jnp.einsum(
            "dszyx,dc->sczyx", voxels, fit_rows, preferred_element_type=jnp.float32
        ).astype(jnp.bfloat16)
        kept, got = coeffs[0], coeffs[1]
        far_a = lax.ppermute(kept, "gz", away)
        far_b = lax.ppermute(got, "gz", across)
        flags = jnp.stack([odd, part])
        mine, other = filter_call(flags, back, (far_a, far_b, kept, got))
        other = scoped(f"back{chunk}", other, "gz", pair)
        for side, piece in ((odd, mine), (1 - odd, other)):
            for hop in range(parts):
                block = piece
                if hop:
                    block = lax.ppermute(
                        piece, "dir", [(i, (i + hop) % parts) for i in range(parts)]
                    )
                number = lax.rem(part - hop + parts, parts)
                number = side * (half // strip) + chunk * parts + number
                made = jnp.einsum(
                    "czyx,cd->dzyx", block, own_basis, preferred_element_type=jnp.float32
                ).astype(jnp.bfloat16)
                if strip % 8:
                    outs = (lax.dynamic_update_slice_in_dim(outs[0], made, number * strip, 2),)
                else:
                    outs = finish_call(number.reshape(1), made, estimate, outs)
    if strip % 8:
        correction = outs[0]
        updated = (
            estimate.astype(jnp.float32) + STEP_SIZE * correction.astype(jnp.float32)
        ).astype(jnp.bfloat16)
        return (correction, updated)
    return tuple(outs)


def solution(mesh):
    return jax.shard_map(
        shards,
        mesh=mesh,
        in_specs=(
            P("dir", "gz", "gy", None),
            P("dir", "gz", "gy", None),
            P(),
            P(),
            P(),
            P(None, "dir"),
            P(),
            P(),
        ),
        out_specs=(P("dir", "gz", "gy", None), P("dir", "gz", "gy", None)),
        check_vma=False,
    )
```
